256 devices in a mesh: row: 16 (over z, y_hi), col: 16 (over y_lo, x, core).
Axes of the slice: x: 4, y: 4 (y_hi: 2, y_lo: 2; y = y_hi * 2 + y_lo), z: 8, core: 2. Of those that a mesh axis runs over, the one named last changes fastest.
Arguments:
- source: float32 [131072, 512], P(('row', 'col')), may hold values from -1.3 to 1.3
- context: float32 [131072, 512], P(('row', 'col')), may hold values from -1.3 to 1.3
- pair_counts: int32 [4, 131072, 512], P(None, ('row', 'col')), may hold values from 0 to 4
- partner_masks: int32 [4], replicated, may hold values from 1 to 15, as said below
Outputs:
- source_out: float32 [131072, 512], P(('row', 'col'))
- context_out: float32 [131072, 512], P(('row', 'col'))
The draws below stay inside these ranges and needn't reach their ends.
Inputs may be any that keep to these rules, and one draw needn't show every extreme that they name: `partner_masks`: entry k is the offset of round k: for even k it is below 16, for odd k below 16; never zero.
All inputs are finite; a program needn't handle non-finite values.
Results may differ from the reference program's by a relative error of at most 0.0019.
Values sent between devices are 32-bit elements; how exact they have to be, the bound alone decides.
A program may use at most 128 MiB of HBM per device.

```python
import jax
import jax.numpy as jnp
from jax import lax

D = 512
SRC_DEV = 512
CTX_DEV = 512
ROUNDS = 4
SOURCES = 131072
CONTEXTS = 131072
N_ROW = 16
N_COL = 16


def draw_source(key, part):
    entry_key = jax.random.fold_in(key, 11)
    values = jnp.clip(jax.random.normal(entry_key, (SOURCES, D), jnp.float32), -6.0, 6.0) * 0.21
    return values.astype(jnp.float32)


def draw_context(key, part):
    entry_key = jax.random.fold_in(key, 12)
    values = jnp.clip(jax.random.normal(entry_key, (CONTEXTS, D), jnp.float32), -6.0, 6.0) * 0.21
    return values.astype(jnp.float32)


def draw_partner_masks(key, part):
    turns = jnp.arange(ROUNDS, dtype=jnp.int32)
    limits = jnp.where(turns % 2 == 0, N_ROW, N_COL).astype(jnp.int32)
    raw_bits = jax.random.randint(jax.random.fold_in(key, 13), (ROUNDS,), 0, 1048576, jnp.int32)
    offsets = (1 + raw_bits % (limits - 1)).astype(jnp.int32)
    biggest = jnp.max(limits)
    pick_bits = jax.random.randint(jax.random.fold_in(key, 14), (ROUNDS,), 0, 1048576, jnp.int32)
    scores = jnp.where(limits == biggest, pick_bits * ROUNDS + turns, -1).astype(jnp.int32)
    chosen = lax.top_k(scores, 1)[1][0].astype(jnp.int32)
    offsets = jnp.where(turns == chosen, limits - 1, offsets)
    return offsets.astype(jnp.int32)


def with_ends(result, own_key, least, high):
    longest = result.shape.index(max(result.shape))
    spots = []
    for shift in (0, 1):
        where = [jax.random.randint(jax.random.fold_in(own_key, axis), (), 0, length) for axis, length in enumerate(result.shape)]
        where[longest] = (where[longest] + shift) % result.shape[longest]
        spots.append(tuple(where))
    return result.at[spots[0]].set(least).at[spots[1]].set(high)


def setup_inputs(seed: int = 0) -> dict:
    seeds = jax.random.split(jax.random.key(seed), 5)
    return {
        "source": draw_source(jax.random.fold_in(seeds[4], 71), 0),
        "context": draw_context(jax.random.fold_in(seeds[4], 71), 0),
        "pair_counts": with_ends(jax.random.randint(seeds[2], (ROUNDS, SOURCES, CTX_DEV), 0, 5), jax.random.fold_in(seeds[2], 1), 0, 4).astype(jnp.int32),
        "partner_masks": draw_partner_masks(jax.random.fold_in(seeds[4], 71), 0),
    }


LEARN_RATE = 0.05
NEG_WEIGHT = 1.0
EPSILON = 1e-06

def rounded(values):
    half = lax.optimization_barrier(values.astype(jnp.bfloat16))
    return half.astype(jnp.float32)

def normalized(param, grad):
    scale = lax.rsqrt(lax.optimization_barrier(jnp.mean(grad * grad, axis=1, keepdims=True)) + EPSILON)
    return param - LEARN_RATE * grad * scale

def train_pair(operands):
    src_block, ctx_block, tile = operands
    src_low = rounded(src_block)
    ctx_low = rounded(ctx_block)
    scores = jnp.dot(src_low, ctx_low.T, preferred_element_type=jnp.float32, precision=lax.Precision.HIGHEST)
    weight = tile.astype(jnp.float32)
    coef = rounded((weight + NEG_WEIGHT) * jax.nn.sigmoid(scores) - weight)
    grad_src = jnp.dot(coef, ctx_low, preferred_element_type=jnp.float32, precision=lax.Precision.HIGHEST)
    grad_ctx = jnp.dot(coef.T, src_low, preferred_element_type=jnp.float32, precision=lax.Precision.HIGHEST)
    return (normalized(src_block, grad_src), normalized(ctx_block, grad_ctx))

def reference(source, context, pair_counts, partner_masks):
    blocks = N_ROW * N_COL
    sources = source.reshape(blocks, SRC_DEV, D)
    contexts = context.reshape(blocks, CTX_DEV, D)
    row_ids = jnp.repeat(jnp.arange(N_ROW, dtype=jnp.int32), N_COL)
    col_ids = jnp.tile(jnp.arange(N_COL, dtype=jnp.int32), N_ROW)
    row_total = jnp.zeros((), jnp.int32)
    col_total = jnp.zeros((), jnp.int32)
    for turn in range(ROUNDS):
        if turn % 2 == 0:
            row_total = (row_total + partner_masks[turn].astype(jnp.int32)) % N_ROW
        else:
            col_total = (col_total + partner_masks[turn].astype(jnp.int32)) % N_COL
        partner = ((row_ids + row_total) % N_ROW * N_COL + (col_ids + col_total) % N_COL).astype(jnp.int32)
        tiles = pair_counts[turn].reshape(blocks, SRC_DEV, CTX_DEV)
        met = contexts[partner]
        new_src, new_met = lax.map(train_pair, (sources, met, tiles))
        sources = new_src
        contexts = contexts.at[partner].set(new_met)
    return (sources.reshape(SOURCES, D), contexts.reshape(CONTEXTS, D))
```

```python
import functools

import jax
import jax.numpy as jnp
from jax import lax
from jax.experimental import pallas as pl
from jax.experimental.pallas import tpu as pltpu
from jax.sharding import PartitionSpec as P

LEARN_RATE = 0.05
NEG_WEIGHT = 1.0
EPSILON = 1e-06
MESH = pl.DeviceIdType.MESH
ROWS = 16
COLS = 16
GROUP = 128
PIECES = 8


def normalized(param, grad):
    scale = lax.rsqrt(jnp.mean(grad * grad, axis=1, keepdims=True) + EPSILON)
    return param - LEARN_RATE * grad * scale


def place(axis, by):
    row, col = lax.axis_index("row"), lax.axis_index("col")
    if axis == "row":
        return (lax.rem(row + by % ROWS, ROWS), col)
    return (row, lax.rem(col + by % COLS, COLS))


def source_update(src_ref, coef_ref, low_ref, src_out):
    size = src_ref.shape[0]

    def step(i, carry):
        rows = pl.ds(pl.multiple_of(i * GROUP, GROUP), GROUP)
        grad = jnp.dot(coef_ref[rows, :], low_ref[...], preferred_element_type=jnp.float32)
        src_out[rows, :] = normalized(src_ref[rows, :], grad)
        return carry

    lax.fori_loop(0, size // GROUP, step, 0)


def round_kernel(axis, by, turn, first, *refs):
    if first:
        ctx_ref, src_in, counts, ctx_out, coef_out, low_out = refs[:6]
        land, weight, src_low, send, recv, wsem = refs[6:]
        src_out = src_in
    else:
        ctx_ref, src_in, coef_in, low_in, counts, ctx_out, src_out, coef_out, low_out = refs[:9]
        land, weight, src_low, send, recv, wsem = refs[9:]
    size = ctx_ref.shape[0]
    piece = size // PIECES
    barrier = pltpu.get_barrier_semaphore()
    pl.semaphore_signal(barrier, inc=1, device_id=place(axis, by), device_id_type=MESH)
    fetch = pltpu.make_async_copy(counts.at[turn], weight, wsem)
    fetch.start()
    pl.semaphore_wait(barrier, 1)

    def move(i):
        rows = pl.ds(pl.multiple_of(i * piece, piece), piece)
        return pltpu.make_async_remote_copy(
            src_ref=ctx_ref.at[rows],
            dst_ref=land.at[rows],
            send_sem=send.at[i],
            recv_sem=recv.at[i],
            device_id=place(axis, -by),
            device_id_type=MESH,
        )

    def launch(i, carry):
        move(i).start()
        return carry

    lax.fori_loop(0, PIECES, launch, 0)
    if not first:
        source_update(src_in, coef_in, low_in, src_out)
    src_low[...] = src_out[...].astype(jnp.bfloat16)
    fetch.wait()

    def group(g, carry):
        for k in range(GROUP // piece):
            move(g * (GROUP // piece) + k).wait_recv()
        rows = pl.ds(pl.multiple_of(g * GROUP, GROUP), GROUP)
        ctx = land[rows, :]
        low = ctx.astype(jnp.bfloat16)
        low_out[rows, :] = low
        scores = lax.dot_general(
            src_low[...], low, (((1,), (1,)), ((), ())), preferred_element_type=jnp.float32
        )
        count = weight[:, rows].astype(jnp.float32)
        coef = ((count + NEG_WEIGHT) * jax.nn.sigmoid(scores) - count).astype(jnp.bfloat16)
        coef_out[:, rows] = coef
        grad = lax.dot_general(
            coef, src_low[...], (((0,), (0,)), ((), ())), preferred_element_type=jnp.float32
        )
        ctx_out[rows, :] = normalized(ctx, grad)
        return carry

    lax.fori_loop(0, size // GROUP, group, 0)

    def sent(i, carry):
        move(i).wait_send()
        return carry

    lax.fori_loop(0, PIECES, sent, 0)


def one_round(axis, by, turn, number, ctx, src, coef, low, counts):
    first = coef is None
    size, width = ctx.shape
    vmem = pl.BlockSpec(memory_space=pltpu.VMEM)
    hbm = pl.BlockSpec(memory_space=pl.ANY)
    full = jax.ShapeDtypeStruct((size, width), jnp.float32)
    coef_shape = jax.ShapeDtypeStruct((src.shape[0], size), jnp.bfloat16)
    low_shape = jax.ShapeDtypeStruct((size, width), jnp.bfloat16)
    out = (full, coef_shape, low_shape) if first else (full, full, coef_shape, low_shape)
    args = (ctx, src, counts) if first else (ctx, src, coef, low, counts)
    return pl.pallas_call(
        functools.partial(round_kernel, axis, by, turn, first),
        out_shape=out,
        in_specs=[vmem] * (len(args) - 1) + [hbm],
        out_specs=[vmem] * len(out),
        scratch_shapes=[
            pltpu.VMEM((size, width), jnp.float32),
            pltpu.VMEM((src.shape[0], size), jnp.int32),
            pltpu.VMEM(src.shape, jnp.bfloat16),
            pltpu.SemaphoreType.DMA((PIECES,)),
            pltpu.SemaphoreType.DMA((PIECES,)),
            pltpu.SemaphoreType.DMA,
        ],
        name=f"round{turn}_{axis}{by}",
        compiler_params=pltpu.CompilerParams(
            collective_id=number, has_side_effects=True, vmem_limit_bytes=24 << 20
        ),
    )(*args)


QUARTERS = 4


def return_kernel(by, total, ctx_ref, src_in, coef_in, low_in, ctx_out, src_out, *scratch):
    near = scratch[:QUARTERS]
    stage = scratch[QUARTERS : 2 * QUARTERS]
    far = scratch[2 * QUARTERS : 3 * QUARTERS]
    send1, recv1, send2, recv2 = scratch[3 * QUARTERS :]
    size, width = ctx_ref.shape
    quarter = size // QUARTERS
    piece = quarter // COLS
    row, col = lax.axis_index("row"), lax.axis_index("col")

    def wrap(value, length):
        return lax.rem(value + length, length)

    barrier = pltpu.get_barrier_semaphore()

    def greet(i, carry):
        pl.semaphore_signal(
            barrier, inc=1, device_id=(wrap(row - by, ROWS), wrap(col - i, COLS)), device_id_type=MESH
        )
        return carry

    def greet_col(i, carry):
        pl.semaphore_signal(
            barrier, inc=1, device_id=(row, wrap(col - i, COLS)), device_id_type=MESH
        )
        return carry

    start = 0 if by else 1
    lax.fori_loop(start, COLS, greet, 0)
    if by:
        lax.fori_loop(1, COLS, greet_col, 0)
    pl.semaphore_wait(barrier, COLS - start + (COLS - 1 if by else 0))

    def spread(q, i):
        return pltpu.make_async_remote_copy(
            src_ref=ctx_ref.at[pl.ds(pl.multiple_of(q * quarter + i * piece, piece), piece)],
            dst_ref=near[q].at[i],
            send_sem=send1.at[q],
            recv_sem=recv1.at[q],
            device_id=(wrap(row + by, ROWS), wrap(col + i, COLS)),
            device_id_type=MESH,
        )

    def spread_all(q):
        own = pl.ds(q * quarter + start * piece, quarter - start * piece)
        return pltpu.make_async_remote_copy(
            src_ref=ctx_ref.at[own],
            dst_ref=near[q].at[pl.ds(start, COLS - start)],
            send_sem=send1.at[q],
            recv_sem=recv1.at[q],
            device_id=(wrap(row + by, ROWS), wrap(col + 1, COLS)),
            device_id_type=MESH,
        )

    def deliver_all(q):
        return pltpu.make_async_remote_copy(
            src_ref=stage[q].at[pl.ds(1, COLS - 1)],
            dst_ref=far[q].at[pl.ds(1, COLS - 1)],
            send_sem=send2.at[q],
            recv_sem=recv2.at[q],
            device_id=(row, wrap(col + 1, COLS)),
            device_id_type=MESH,
        )

    def deliver(q, i):
        return pltpu.make_async_remote_copy(
            src_ref=stage[q].at[i],
            dst_ref=far[q].at[i],
            send_sem=send2.at[q],
            recv_sem=recv2.at[q],
            device_id=(row, wrap(col + i, COLS)),
            device_id_type=MESH,
        )

    for q in range(QUARTERS):

        def launch(i, carry, q=q):
            spread(q, i).start()
            return carry

        lax.fori_loop(start, COLS, launch, 0)
        if not by:
            near[q][0] = ctx_ref[pl.ds(q * quarter, piece), :]
    source_update(src_in, coef_in, low_in, src_out)
    shift = total[0]
    for q in range(QUARTERS):

        spread_all(q).wait_recv()
        far[q][0] = near[q][lax.rem(shift, COLS)]

        def pass_on(i, carry, q=q):
            stage[q][i] = near[q][lax.rem(shift - i + COLS, COLS)]
            deliver(q, i).start()
            return carry

        lax.fori_loop(1, COLS, pass_on, 0)
    for q in range(QUARTERS):

        deliver_all(q).wait_recv()

        def settle(i, carry, q=q):
            rows = pl.ds(pl.multiple_of(q * quarter + i * piece, piece), piece)
            ctx_out[rows, :] = far[q][lax.rem(shift - i + COLS, COLS)]
            return carry

        lax.fori_loop(0, COLS, settle, 0)
    for q in range(QUARTERS):

        deliver_all(q).wait_send()
        spread_all(q).wait_send()


def go_home(by, number, total, ctx, src, coef, low):
    size, width = ctx.shape
    quarter = size // QUARTERS
    vmem = pl.BlockSpec(memory_space=pltpu.VMEM)
    full = jax.ShapeDtypeStruct((size, width), jnp.float32)
    slots = pltpu.VMEM((COLS, quarter // COLS, width), jnp.float32)
    return pl.pallas_call(
        functools.partial(return_kernel, by),
        out_shape=(full, full),
        in_specs=[pl.BlockSpec(memory_space=pltpu.SMEM)] + [vmem] * 4,
        out_specs=[vmem] * 2,
        scratch_shapes=[slots] * (3 * QUARTERS) + [pltpu.SemaphoreType.DMA((QUARTERS,))] * 4,
        name=f"home{by}",
        compiler_params=pltpu.CompilerParams(
            collective_id=number, has_side_effects=True, vmem_limit_bytes=24 << 20
        ),
    )(total, ctx, src, coef, low)


def per_device(source, context, pair_counts, partner_masks):
    rounds = pair_counts.shape[0]
    ctx, src, coef, low = context, source, None, None
    number = 0
    for turn in range(rounds):
        axis, length = ("row", ROWS) if turn % 2 == 0 else ("col", COLS)
        branches = []
        for by in range(1, length):
            if coef is None:
                def branch(ctx, src, counts, axis=axis, by=by, turn=turn, number=number):
                    out = one_round(axis, by, turn, number, ctx, src, None, None, counts)
                    return (out[0], src, out[1], out[2])
            else:
                def branch(ctx, src, coef, low, counts, axis=axis, by=by, turn=turn, number=number):
                    return tuple(one_round(axis, by, turn, number, ctx, src, coef, low, counts))
            branches.append(branch)
            number += 1
        args = (ctx, src, pair_counts) if coef is None else (ctx, src, coef, low, pair_counts)
        ctx, src, coef, low = lax.switch(partner_masks[turn] - 1, branches, *args)
    row_total = sum(partner_masks[turn] for turn in range(0, rounds, 2)) % ROWS
    col_total = sum(partner_masks[turn] for turn in range(1, rounds, 2)) % COLS
    branches = [functools.partial(go_home, by, number + by) for by in range(ROWS)]
    ctx, src = lax.switch(row_total, branches, col_total.reshape(1), ctx, src, coef, low)
    return (src, ctx)


def solution(mesh):
    in_specs = (
        P(("row", "col"), None),
        P(("row", "col"), None),
        P(None, ("row", "col"), None),
        P(),
    )
    out_specs = (P(("row", "col"), None), P(("row", "col"), None))
    return jax.shard_map(
        per_device, mesh=mesh, in_specs=in_specs, out_specs=out_specs, check_vma=False
    )
```

```python
import functools

import jax
import jax.numpy as jnp
from jax import lax
from jax.experimental import pallas as pl
from jax.experimental.pallas import tpu as pltpu
from jax.sharding import PartitionSpec as P

LEARN_RATE = 0.05
NEG_WEIGHT = 1.0
EPSILON = 1e-06
MESH = pl.DeviceIdType.MESH
ROWS = 16
COLS = 16
GROUP = 128
PIECES = 8
STRIP = 64


def normalized(param, grad):
    scale = lax.rsqrt(jnp.mean(grad * grad, axis=1, keepdims=True) + EPSILON)
    return param - LEARN_RATE * grad * scale


def place(axis, by):
    row, col = lax.axis_index("row"), lax.axis_index("col")
    if axis == "row":
        return (lax.rem(row + by % ROWS, ROWS), col)
    return (row, lax.rem(col + by % COLS, COLS))


def tiles(count, body):
    def step(i, carry):
        body(i)
        return carry

    lax.fori_loop(0, count, step, 0)


def block(i, size):
    return pl.ds(pl.multiple_of(i * size, size), size)


def source_update(src_ref, coef_ref, low_ref, src_out):
    def step(i):
        rows = block(i, STRIP)
        grad = jnp.dot(coef_ref[rows, :], low_ref[...], preferred_element_type=jnp.float32)
        src_out[rows, :] = normalized(src_ref[rows, :], grad)

    tiles(src_ref.shape[0] // STRIP, step)


def round_kernel(
    axis,
    by,
    turns,
    lap_ref,
    ctx_ref,
    src_in,
    coef_in,
    low_in,
    counts,
    ctx_out,
    src_out,
    coef_out,
    low_out,
    land,
    weight,
    src_low,
    grad_ref,
    send,
    recv,
    wsem,
):
    size = ctx_ref.shape[0]
    piece = size // PIECES
    barrier = pltpu.get_barrier_semaphore()
    pl.semaphore_signal(barrier, inc=1, device_id=place(axis, by), device_id_type=MESH)
    fetches = [
        pltpu.make_async_copy(counts.at[turn], weight.at[lap], wsem.at[lap])
        for lap, turn in enumerate(turns)
    ]
    for fetch in fetches:
        fetch.start()
    pl.semaphore_wait(barrier, 1)

    def move(i):
        rows = pl.ds(pl.multiple_of(i * piece, piece), piece)
        return pltpu.make_async_remote_copy(
            src_ref=ctx_ref.at[rows],
            dst_ref=land.at[rows],
            send_sem=send.at[i],
            recv_sem=recv.at[i],
            device_id=place(axis, -by),
            device_id_type=MESH,
        )

    tiles(PIECES, lambda i: move(i).start())
    source_update(src_in, coef_in, low_in, src_out)

    def narrow(i):
        rows = block(i, STRIP)
        src_low[rows, :] = src_out[rows, :].astype(jnp.bfloat16)

    tiles(size // STRIP, narrow)
    for fetch in fetches:
        fetch.wait()
    lap = lap_ref[0]

    def group(g):
        for k in range(GROUP // piece):
            move(g * (GROUP // piece) + k).wait_recv()
        rows = block(g, GROUP)
        low_out[rows, :] = land[rows, :].astype(jnp.bfloat16)

        def score(i):
            strip = block(i, STRIP)
            scores = lax.dot_general(
                src_low[strip, :],
                low_out[rows, :],
                (((1,), (1,)), ((), ())),
                preferred_element_type=jnp.float32,
            )
            count = weight[lap, strip, rows].astype(jnp.float32)
            coef = (count + NEG_WEIGHT) * jax.nn.sigmoid(scores) - count
            coef_out[strip, rows] = coef.astype(jnp.bfloat16)

        tiles(src_low.shape[0] // STRIP, score)
        grad_ref[...] = lax.dot_general(
            coef_out[:, rows],
            src_low[...],
            (((0,), (0,)), ((), ())),
            preferred_element_type=jnp.float32,
        )

        def update(i):
            strip = pl.ds(pl.multiple_of(g * GROUP + i * 32, 32), 32)
            ctx_out[strip, :] = normalized(land[strip, :], grad_ref[block(i, 32), :])

        tiles(GROUP // 32, update)

    tiles(size // GROUP, group)
    tiles(PIECES, lambda i: move(i).wait_send())


def one_round(axis, by, turns, number, lap, ctx, src, coef, low, counts):
    size, width = ctx.shape
    vmem = pl.BlockSpec(memory_space=pltpu.VMEM)
    out = [jax.ShapeDtypeStruct(x.shape, x.dtype) for x in (ctx, src, coef, low)]
    return pl.pallas_call(
        functools.partial(round_kernel, axis, by, turns),
        out_shape=tuple(out),
        in_specs=[pl.BlockSpec(memory_space=pltpu.SMEM)]
        + [vmem] * 4
        + [pl.BlockSpec(memory_space=pl.ANY)],
        out_specs=[vmem] * 4,
        scratch_shapes=[
            pltpu.VMEM((size, width), jnp.float32),
            pltpu.VMEM((len(turns), src.shape[0], size), jnp.int32),
            pltpu.VMEM(src.shape, jnp.bfloat16),
            pltpu.VMEM((GROUP, width), jnp.float32),
            pltpu.SemaphoreType.DMA((PIECES,)),
            pltpu.SemaphoreType.DMA((PIECES,)),
            pltpu.SemaphoreType.DMA((len(turns),)),
        ],
        name=f"round_{axis}{by}",
        compiler_params=pltpu.CompilerParams(
            collective_id=number, has_side_effects=True, vmem_limit_bytes=24 << 20
        ),
    )(lap, ctx, src, coef, low, counts)


QUARTERS = 4


def return_kernel(by, total, ctx_ref, src_in, coef_in, low_in, ctx_out, src_out, *scratch):
    near = scratch[:QUARTERS]
    stage = scratch[QUARTERS : 2 * QUARTERS]
    far = scratch[2 * QUARTERS : 3 * QUARTERS]
    send1, recv1, send2, recv2 = scratch[3 * QUARTERS :]
    size, width = ctx_ref.shape
    quarter = size // QUARTERS
    piece = quarter // COLS
    row, col = lax.axis_index("row"), lax.axis_index("col")

    def wrap(value, length):
        return lax.rem(value + length, length)

    barrier = pltpu.get_barrier_semaphore()

    def greet(i, carry):
        pl.semaphore_signal(
            barrier, inc=1, device_id=(wrap(row - by, ROWS), wrap(col - i, COLS)), device_id_type=MESH
        )
        return carry

    def greet_col(i, carry):
        pl.semaphore_signal(
            barrier, inc=1, device_id=(row, wrap(col - i, COLS)), device_id_type=MESH
        )
        return carry

    start = 0 if by else 1
    lax.fori_loop(start, COLS, greet, 0)
    if by:
        lax.fori_loop(1, COLS, greet_col, 0)
    pl.semaphore_wait(barrier, COLS - start + (COLS - 1 if by else 0))

    def spread(q, i):
        return pltpu.make_async_remote_copy(
            src_ref=ctx_ref.at[pl.ds(pl.multiple_of(q * quarter + i * piece, piece), piece)],
            dst_ref=near[q].at[i],
            send_sem=send1.at[q],
            recv_sem=recv1.at[q],
            device_id=(wrap(row + by, ROWS), wrap(col + i, COLS)),
            device_id_type=MESH,
        )

    def spread_all(q):
        own = pl.ds(q * quarter + start * piece, quarter - start * piece)
        return pltpu.make_async_remote_copy(
            src_ref=ctx_ref.at[own],
            dst_ref=near[q].at[pl.ds(start, COLS - start)],
            send_sem=send1.at[q],
            recv_sem=recv1.at[q],
            device_id=(wrap(row + by, ROWS), wrap(col + 1, COLS)),
            device_id_type=MESH,
        )

    def deliver_all(q):
        return pltpu.make_async_remote_copy(
            src_ref=stage[q].at[pl.ds(1, COLS - 1)],
            dst_ref=far[q].at[pl.ds(1, COLS - 1)],
            send_sem=send2.at[q],
            recv_sem=recv2.at[q],
            device_id=(row, wrap(col + 1, COLS)),
            device_id_type=MESH,
        )

    def deliver(q, i):
        return pltpu.make_async_remote_copy(
            src_ref=stage[q].at[i],
            dst_ref=far[q].at[i],
            send_sem=send2.at[q],
            recv_sem=recv2.at[q],
            device_id=(row, wrap(col + i, COLS)),
            device_id_type=MESH,
        )

    def begin(q):
        tiles(COLS - start, lambda i: spread(q, i + start).start())
        if not by:
            near[q][0] = ctx_ref[pl.ds(q * quarter, piece), :]

    begin(0)
    begin(1)
    source_update(src_in, coef_in, low_in, src_out)
    shift = total[0]
    for q in range(QUARTERS):
        spread_all(q).wait_recv()
        if q + 2 < QUARTERS:
            begin(q + 2)
        far[q][0] = near[q][lax.rem(shift, COLS)]

        def pass_on(i, q=q):
            stage[q][i + 1] = near[q][lax.rem(shift - i - 1 + COLS, COLS)]
            deliver(q, i + 1).start()

        tiles(COLS - 1, pass_on)
    for q in range(QUARTERS):
        deliver_all(q).wait_recv()

        def settle(i, q=q):
            rows = pl.ds(pl.multiple_of(q * quarter + i * piece, piece), piece)
            ctx_out[rows, :] = far[q][lax.rem(shift - i + COLS, COLS)]

        tiles(COLS, settle)
    for q in range(QUARTERS):
        deliver_all(q).wait_send()
        spread_all(q).wait_send()


def go_home(by, number, total, ctx, src, coef, low):
    size, width = ctx.shape
    quarter = size // QUARTERS
    vmem = pl.BlockSpec(memory_space=pltpu.VMEM)
    full = jax.ShapeDtypeStruct((size, width), jnp.float32)
    slots = pltpu.VMEM((COLS, quarter // COLS, width), jnp.float32)
    return pl.pallas_call(
        functools.partial(return_kernel, by),
        out_shape=(full, full),
        in_specs=[pl.BlockSpec(memory_space=pltpu.SMEM)] + [vmem] * 4,
        out_specs=[vmem] * 2,
        scratch_shapes=[slots] * (3 * QUARTERS) + [pltpu.SemaphoreType.DMA((QUARTERS,))] * 4,
        name=f"home{by}",
        compiler_params=pltpu.CompilerParams(
            collective_id=number, has_side_effects=True, vmem_limit_bytes=24 << 20
        ),
    )(total, ctx, src, coef, low)


def per_device(source, context, pair_counts, partner_masks):
    rounds = pair_counts.shape[0]

    def both(lap, carried):
        for half, (axis, length) in enumerate((("row", ROWS), ("col", COLS))):
            branches = [
                functools.partial(
                    one_round, axis, by, range(half, rounds, 2), half * ROWS + by
                )
                for by in range(1, length)
            ]
            carried = lax.switch(
                partner_masks[2 * lap + half] - 1,
                branches,
                lap.reshape(1),
                *carried,
                pair_counts,
            )
        return tuple(carried)

    coef = jnp.zeros((source.shape[0], context.shape[0]), jnp.bfloat16)
    low = jnp.zeros(context.shape, jnp.bfloat16)
    ctx, src, coef, low = lax.fori_loop(0, rounds // 2, both, (context, source, coef, low))
    row_total = sum(partner_masks[turn] for turn in range(0, rounds, 2)) % ROWS
    col_total = sum(partner_masks[turn] for turn in range(1, rounds, 2)) % COLS
    branches = [functools.partial(go_home, by, 2 * ROWS + by) for by in range(ROWS)]
    ctx, src = lax.switch(row_total, branches, col_total.reshape(1), ctx, src, coef, low)
    return (src, ctx)


def solution(mesh):
    in_specs = (
        P(("row", "col"), None),
        P(("row", "col"), None),
        P(None, ("row", "col"), None),
        P(),
    )
    out_specs = (P(("row", "col"), None), P(("row", "col"), None))
    return jax.shard_map(
        per_device, mesh=mesh, in_specs=in_specs, out_specs=out_specs, check_vma=False
    )
```

```python
import functools

import jax
import jax.numpy as jnp
from jax import lax
from jax.experimental import pallas as pl
from jax.experimental.pallas import tpu as pltpu
from jax.sharding import PartitionSpec as P

LEARN_RATE = 0.05
NEG_WEIGHT = 1.0
EPSILON = 1e-06
MESH = pl.DeviceIdType.MESH
ROWS = 16
COLS = 16
GROUP = 128
PIECES = 16
STRIP = 64


def normalized(param, grad):
    scale = lax.rsqrt(jnp.mean(grad * grad, axis=1, keepdims=True) + EPSILON)
    return param - LEARN_RATE * grad * scale


def place(axis, by):
    row, col = lax.axis_index("row"), lax.axis_index("col")
    if axis == "row":
        return (lax.rem(row + by + ROWS, ROWS), col)
    return (row, lax.rem(col + by + COLS, COLS))


class Detour:
    def __init__(self, shift, parts):
        counts, first, second = [], [], []
        for odd in range(2):
            hops = ((odd + shift) // 2) % 8
            hops = hops - 8 if hops > 4 else hops
            sign = 1 if hops > 0 else -1
            leg = {2: -3 * sign, 3: -2 * sign}.get(abs(hops), 0)
            counts.append({2: parts[0], 3: parts[1]}.get(abs(hops), 0))
            first.append(2 * leg % ROWS)
            second.append((shift - 2 * leg) % ROWS)
        self.shift, self.counts, self.first, self.second = shift, counts, first, second
        self.any = max(counts) > 0

    @staticmethod
    def pick(values, odd):
        return values[0] if values[0] == values[1] else values[0] + (values[1] - values[0]) * odd


def tiles(count, body):
    def step(i, carry):
        body(i)
        return carry

    lax.fori_loop(0, count, step, 0)


def block(i, size):
    return pl.ds(pl.multiple_of(i * size, size), size)


def source_update(src_ref, coef_ref, low_ref, src_out):
    def step(i):
        rows = block(i, STRIP)
        grad = jnp.dot(coef_ref[rows, :], low_ref[...], preferred_element_type=jnp.float32)
        src_out[rows, :] = normalized(src_ref[rows, :], grad)

    tiles(src_ref.shape[0] // STRIP, step)


def as_flag(count):
    return jnp.minimum(count, 1)


def detour_of(axis, by):
    if axis != "row":
        return None
    detour = Detour(-by, (4, 6))
    return detour if detour.any else None


def round_kernel(
    axis,
    by,
    turns,
    lap_ref,
    ctx_ref,
    src_in,
    coef_in,
    low_in,
    counts,
    ctx_out,
    src_out,
    coef_out,
    low_out,
    land,
    weight,
    src_low,
    grad_ref,
    send,
    recv,
    wsem,
    hop=None,
    hop_send=None,
    hop_recv=None,
):
    size = ctx_ref.shape[0]
    piece = size // PIECES
    fetches = [
        pltpu.make_async_copy(counts.at[turn], weight.at[lap], wsem.at[lap])
        for lap, turn in enumerate(turns)
    ]
    for fetch in fetches:
        fetch.start()
    detour = detour_of(axis, by)
    barrier = pltpu.get_barrier_semaphore()

    def greet(there):
        pl.semaphore_signal(barrier, inc=1, device_id=there, device_id_type=MESH)

    greet(place(axis, by))
    long = 0
    if detour is None:
        pl.semaphore_wait(barrier, 1)
    else:
        odd = lax.rem(lax.axis_index("row"), 2)
        origin = lax.rem(odd + by, 2)
        long = detour.pick(detour.counts, odd)
        first, second = detour.pick(detour.first, odd), detour.pick(detour.second, odd)
        tiles(as_flag(long), lambda i: greet(place(axis, ROWS - first)))
        tiles(
            as_flag(detour.pick(detour.counts, origin)),
            lambda i: greet(place(axis, ROWS - detour.pick(detour.second, origin))),
        )
        pl.semaphore_wait(barrier, 1 + 2 * as_flag(long))

    def move(i):
        rows = pl.ds(pl.multiple_of(i * piece, piece), piece)
        return pltpu.make_async_remote_copy(
            src_ref=ctx_ref.at[rows],
            dst_ref=land.at[rows],
            send_sem=send.at[i],
            recv_sem=recv.at[i],
            device_id=place(axis, -by),
            device_id_type=MESH,
        )

    def depart(i):
        return pltpu.make_async_remote_copy(
            src_ref=ctx_ref.at[block(PIECES - long + i, piece)],
            dst_ref=hop.at[block(i, piece)],
            send_sem=send.at[PIECES - long + i],
            recv_sem=hop_recv.at[i],
            device_id=place(axis, first),
            device_id_type=MESH,
        )

    def forward(i):
        return pltpu.make_async_remote_copy(
            src_ref=hop.at[block(i, piece)],
            dst_ref=land.at[block(PIECES - long + i, piece)],
            send_sem=hop_send.at[i],
            recv_sem=recv.at[PIECES - long + i],
            device_id=place(axis, second),
            device_id_type=MESH,
        )

    if detour is not None:
        tiles(long, lambda i: depart(i).start())
    tiles(PIECES - long, lambda i: move(i).start())
    source_update(src_in, coef_in, low_in, src_out)

    def narrow(i):
        rows = block(i, STRIP)
        src_low[rows, :] = src_out[rows, :].astype(jnp.bfloat16)

    tiles(size // STRIP, narrow)
    for fetch in fetches:
        fetch.wait()
    lap = lap_ref[0]

    def group(g):
        tiles(GROUP // piece, lambda k: move(g * (GROUP // piece) + k).wait_recv())
        rows = block(g, GROUP)
        low_out[rows, :] = land[rows, :].astype(jnp.bfloat16)

        def score(i):
            strip = block(i, STRIP)
            scores = lax.dot_general(
                src_low[strip, :],
                low_out[rows, :],
                (((1,), (1,)), ((), ())),
                preferred_element_type=jnp.float32,
            )
            count = weight[lap, strip, rows].astype(jnp.float32)
            coef = (count + NEG_WEIGHT) * jax.nn.sigmoid(scores) - count
            coef_out[strip, rows] = coef.astype(jnp.bfloat16)

        tiles(src_low.shape[0] // STRIP, score)
        grad_ref[...] = lax.dot_general(
            coef_out[:, rows],
            src_low[...],
            (((0,), (0,)), ((), ())),
            preferred_element_type=jnp.float32,
        )

        def update(i):
            strip = pl.ds(pl.multiple_of(g * GROUP + i * 32, 32), 32)
            ctx_out[strip, :] = normalized(land[strip, :], grad_ref[block(i, 32), :])

        tiles(GROUP // 32, update)

    if detour is not None:

        def relay(i):
            depart(i).wait_recv()
            forward(i).start()

        tiles(long, relay)
    tiles(size // GROUP, group)
    tiles(PIECES, lambda i: move(i).wait_send())
    if detour is not None:
        tiles(long, lambda i: forward(i).wait_send())


def one_round(axis, by, turns, number, lap, ctx, src, coef, low, counts):
    size, width = ctx.shape
    vmem = pl.BlockSpec(memory_space=pltpu.VMEM)
    out = [jax.ShapeDtypeStruct(x.shape, x.dtype) for x in (ctx, src, coef, low)]
    detour = detour_of(axis, by)
    detour_scratch = []
    if detour is not None:
        most = max(detour.counts)
        detour_scratch = [
            pltpu.VMEM((most * (size // PIECES), width), jnp.float32),
            pltpu.SemaphoreType.DMA((most,)),
            pltpu.SemaphoreType.DMA((most,)),
        ]
    return pl.pallas_call(
        functools.partial(round_kernel, axis, by, turns),
        out_shape=tuple(out),
        in_specs=[pl.BlockSpec(memory_space=pltpu.SMEM)]
        + [vmem] * 4
        + [pl.BlockSpec(memory_space=pl.ANY)],
        out_specs=[vmem] * 4,
        scratch_shapes=[
            pltpu.VMEM((size, width), jnp.float32),
            pltpu.VMEM((len(turns), src.shape[0], size), jnp.int32),
            pltpu.VMEM(src.shape, jnp.bfloat16),
            pltpu.VMEM((GROUP, width), jnp.float32),
            pltpu.SemaphoreType.DMA((PIECES,)),
            pltpu.SemaphoreType.DMA((PIECES,)),
            pltpu.SemaphoreType.DMA((len(turns),)),
        ]
        + detour_scratch,
        name=f"round_{axis}{by}",
        compiler_params=pltpu.CompilerParams(
            collective_id=number, has_side_effects=True, vmem_limit_bytes=24 << 20
        ),
    )(lap, ctx, src, coef, low, counts)


QUARTERS = 4


def home_detour(by):
    detour = Detour(by, (COLS, COLS + COLS // 2))
    return detour if detour.any else None


def return_kernel(by, total, ctx_ref, src_in, coef_in, low_in, ctx_out, src_out, *scratch):
    near = scratch[:QUARTERS]
    stage = scratch[QUARTERS : 2 * QUARTERS]
    far = scratch[2 * QUARTERS : 3 * QUARTERS]
    send1, recv1, send2, recv2, *detoured = scratch[3 * QUARTERS :]
    size, width = ctx_ref.shape
    quarter = size // QUARTERS
    piece = quarter // COLS
    row, col = lax.axis_index("row"), lax.axis_index("col")

    def at(row_by, col_by):
        return (lax.rem(row + row_by + ROWS, ROWS), lax.rem(col + col_by + COLS, COLS))

    barrier = pltpu.get_barrier_semaphore()

    def greet(there):
        pl.semaphore_signal(barrier, inc=1, device_id=there, device_id_type=MESH)

    start = 0 if by else 1
    tiles(COLS - start, lambda i: greet(at(-by, -i - start)))
    if by:
        tiles(COLS - 1, lambda i: greet(at(0, -i - 1)))
    met = COLS - start + (COLS - 1 if by else 0)
    detour = home_detour(by)
    long = 0
    if detour is not None:
        hop, hop_send, hop_recv = detoured
        odd = lax.rem(row, 2)
        origin = lax.rem(odd + by, 2)
        long = detour.pick(detour.counts, odd)
        first, second = detour.pick(detour.first, odd), detour.pick(detour.second, odd)
        tiles(as_flag(long), lambda i: greet(at(-first, 0)))
        back = detour.pick(detour.second, origin)
        tiles(
            as_flag(detour.pick(detour.counts, origin)) * COLS,
            lambda i: greet(at(-back, -i)),
        )
        met = met + (COLS + 1) * as_flag(long)
    pl.semaphore_wait(barrier, met)

    def spread(q, i):
        return pltpu.make_async_remote_copy(
            src_ref=ctx_ref.at[pl.ds(pl.multiple_of(q * quarter + i * piece, piece), piece)],
            dst_ref=near[q].at[i],
            send_sem=send1.at[q],
            recv_sem=recv1.at[q],
            device_id=at(by, i),
            device_id_type=MESH,
        )

    def spread_all(q):
        own = pl.ds(q * quarter + start * piece, quarter - start * piece)
        return pltpu.make_async_remote_copy(
            src_ref=ctx_ref.at[own],
            dst_ref=near[q].at[pl.ds(start, COLS - start)],
            send_sem=send1.at[q],
            recv_sem=recv1.at[q],
            device_id=at(by, 1),
            device_id_type=MESH,
        )

    def deliver_all(q):
        return pltpu.make_async_remote_copy(
            src_ref=stage[q].at[pl.ds(1, COLS - 1)],
            dst_ref=far[q].at[pl.ds(1, COLS - 1)],
            send_sem=send2.at[q],
            recv_sem=recv2.at[q],
            device_id=at(0, 1),
            device_id_type=MESH,
        )

    def deliver(q, i):
        return pltpu.make_async_remote_copy(
            src_ref=stage[q].at[i],
            dst_ref=far[q].at[i],
            send_sem=send2.at[q],
            recv_sem=recv2.at[q],
            device_id=at(0, i),
            device_id_type=MESH,
        )

    half = quarter // 2

    def depart(q, part):
        return pltpu.make_async_remote_copy(
            src_ref=ctx_ref.at[pl.ds(q * quarter + part * half, half)],
            dst_ref=hop[q % 2].at[pl.ds(part * half, half)],
            send_sem=send1.at[q],
            recv_sem=hop_recv.at[q % 2 * 2 + part],
            device_id=at(first, 0),
            device_id_type=MESH,
        )

    def relay(q, part, i):
        return pltpu.make_async_remote_copy(
            src_ref=hop[q % 2].at[pl.ds(pl.multiple_of(i * piece, piece), piece)],
            dst_ref=near[q].at[i],
            send_sem=hop_send.at[q % 2 * 2 + part],
            recv_sem=recv1.at[q],
            device_id=at(second, i),
            device_id_type=MESH,
        )

    def relayed(q, part):
        return pltpu.make_async_remote_copy(
            src_ref=hop[q % 2].at[pl.ds(part * half, half)],
            dst_ref=near[q].at[pl.ds(part * (COLS // 2), COLS // 2)],
            send_sem=hop_send.at[q % 2 * 2 + part],
            recv_sem=recv1.at[q],
            device_id=at(second, 1),
            device_id_type=MESH,
        )

    ways = []
    if detour is not None:
        ways = [(3, 0, as_flag(long)), (3, 1, as_flag(long)), (2, 1, as_flag(long // (COLS + 1)))]
    for q, part, flag in ways:
        tiles(flag, lambda i, q=q, part=part: depart(q, part).start())
    for q in range(QUARTERS):
        direct = COLS - start
        for other, part, flag in ways:
            if other == q:
                direct = direct - flag * (COLS // 2)
        tiles(direct, lambda i, q=q: spread(q, i + start).start())
        if not by:
            near[q][0] = ctx_ref[pl.ds(q * quarter, piece), :]
    source_update(src_in, coef_in, low_in, src_out)
    for q, part, flag in ways:

        def pass_relay(i, q=q, part=part):
            depart(q, part).wait_recv()
            tiles(COLS // 2, lambda k: relay(q, part, part * (COLS // 2) + k).start())

        tiles(flag, pass_relay)
    shift = total[0]
    for q in range(QUARTERS):
        spread_all(q).wait_recv()
        far[q][0] = near[q][lax.rem(shift, COLS)]

        def pass_on(i, q=q):
            stage[q][i + 1] = near[q][lax.rem(shift - i - 1 + COLS, COLS)]
            deliver(q, i + 1).start()

        tiles(COLS - 1, pass_on)
    for q in range(QUARTERS):
        deliver_all(q).wait_recv()

        def settle(i, q=q):
            rows = pl.ds(pl.multiple_of(q * quarter + i * piece, piece), piece)
            ctx_out[rows, :] = far[q][lax.rem(shift - i + COLS, COLS)]

        tiles(COLS, settle)
    for q in range(QUARTERS):
        deliver_all(q).wait_send()
        spread_all(q).wait_send()
    for q, part, flag in ways:
        tiles(flag, lambda i, q=q, part=part: relayed(q, part).wait_send())


def go_home(by, number, total, ctx, src, coef, low):
    size, width = ctx.shape
    quarter = size // QUARTERS
    vmem = pl.BlockSpec(memory_space=pltpu.VMEM)
    full = jax.ShapeDtypeStruct((size, width), jnp.float32)
    slots = pltpu.VMEM((COLS, quarter // COLS, width), jnp.float32)
    detoured = []
    if home_detour(by) is not None:
        detoured = [
            [pltpu.VMEM((quarter, width), jnp.float32)] * 2,
            pltpu.SemaphoreType.DMA((4,)),
            pltpu.SemaphoreType.DMA((4,)),
        ]
    return pl.pallas_call(
        functools.partial(return_kernel, by),
        out_shape=(full, full),
        in_specs=[pl.BlockSpec(memory_space=pltpu.SMEM)] + [vmem] * 4,
        out_specs=[vmem] * 2,
        scratch_shapes=[slots] * (3 * QUARTERS)
        + [pltpu.SemaphoreType.DMA((QUARTERS,))] * 4
        + detoured,
        name=f"home{by}",
        compiler_params=pltpu.CompilerParams(
            collective_id=number, has_side_effects=True, vmem_limit_bytes=24 << 20
        ),
    )(total, ctx, src, coef, low)


def per_device(source, context, pair_counts, partner_masks):
    rounds = pair_counts.shape[0]

    def both(lap, carried):
        for half, (axis, length) in enumerate((("row", ROWS), ("col", COLS))):
            branches = [
                functools.partial(
                    one_round, axis, by, range(half, rounds, 2), half * ROWS + by
                )
                for by in range(1, length)
            ]
            carried = lax.switch(
                partner_masks[2 * lap + half] - 1,
                branches,
                lap.reshape(1),
                *carried,
                pair_counts,
            )
        return tuple(carried)

    coef = jnp.zeros((source.shape[0], context.shape[0]), jnp.bfloat16)
    low = jnp.zeros(context.shape, jnp.bfloat16)
    ctx, src, coef, low = lax.fori_loop(0, rounds // 2, both, (context, source, coef, low))
    row_total = sum(partner_masks[turn] for turn in range(0, rounds, 2)) % ROWS
    col_total = sum(partner_masks[turn] for turn in range(1, rounds, 2)) % COLS
    branches = [functools.partial(go_home, by, 2 * ROWS + by) for by in range(ROWS)]
    ctx, src = lax.switch(row_total, branches, col_total.reshape(1), ctx, src, coef, low)
    return (src, ctx)


def solution(mesh):
    in_specs = (
        P(("row", "col"), None),
        P(("row", "col"), None),
        P(None, ("row", "col"), None),
        P(),
    )
    out_specs = (P(("row", "col"), None), P(("row", "col"), None))
    return jax.shard_map(
        per_device, mesh=mesh, in_specs=in_specs, out_specs=out_specs, check_vma=False
    )
```

```python
import functools

import jax
import jax.numpy as jnp
from jax import lax
from jax.experimental import pallas as pl
from jax.experimental.pallas import tpu as pltpu
from jax.sharding import PartitionSpec as P

LEARN_RATE = 0.05
NEG_WEIGHT = 1.0
EPSILON = 1e-06
MESH = pl.DeviceIdType.MESH
ROWS = 16
COLS = 16
GROUP = 128
PIECES = 16
STRIP = 64


def normalized(param, grad):
    scale = lax.rsqrt(jnp.mean(grad * grad, axis=1, keepdims=True) + EPSILON)
    return param - LEARN_RATE * grad * scale


def place(axis, by):
    row, col = lax.axis_index("row"), lax.axis_index("col")
    if axis == "row":
        return (lax.rem(row + by + ROWS, ROWS), col)
    return (row, lax.rem(col + by + COLS, COLS))


class Detour:
    def __init__(self, shift, parts):
        counts, first, second = [], [], []
        for odd in range(2):
            hops = ((odd + shift) // 2) % 8
            hops = hops - 8 if hops > 4 else hops
            sign = 1 if hops > 0 else -1
            leg = {2: -3 * sign, 3: -2 * sign}.get(abs(hops), 0)
            counts.append({2: parts[0], 3: parts[1]}.get(abs(hops), 0))
            first.append(2 * leg % ROWS)
            second.append((shift - 2 * leg) % ROWS)
        self.shift, self.counts, self.first, self.second = shift, counts, first, second
        self.any = max(counts) > 0

    @staticmethod
    def pick(values, odd):
        return values[0] if values[0] == values[1] else values[0] + (values[1] - values[0]) * odd


def tiles(count, body):
    def step(i, carry):
        body(i)
        return carry

    lax.fori_loop(0, count, step, 0)


def block(i, size):
    return pl.ds(pl.multiple_of(i * size, size), size)


def source_update(src_ref, coef_ref, low_ref, src_out):
    def step(i):
        rows = block(i, STRIP)
        grad = jnp.dot(coef_ref[rows, :], low_ref[...], preferred_element_type=jnp.float32)
        src_out[rows, :] = normalized(src_ref[rows, :], grad)

    tiles(src_ref.shape[0] // STRIP, step)


def as_flag(count):
    return jnp.minimum(count, 1)


def detour_of(axis, by):
    if axis != "row":
        return None
    detour = Detour(-by, (4, 6))
    return detour if detour.any else None


def round_kernel(
    axis,
    by,
    turns,
    lap_ref,
    ctx_ref,
    src_in,
    coef_in,
    low_in,
    counts,
    ctx_out,
    src_out,
    coef_out,
    low_out,
    land,
    weight,
    src_low,
    grad_ref,
    send,
    recv,
    wsem,
    hop=None,
    hop_send=None,
    hop_recv=None,
):
    size = ctx_ref.shape[0]
    piece = size // PIECES
    fetches = [
        pltpu.make_async_copy(counts.at[turn], weight.at[lap], wsem.at[lap])
        for lap, turn in enumerate(turns)
    ]
    for fetch in fetches:
        fetch.start()
    detour = detour_of(axis, by)
    barrier = pltpu.get_barrier_semaphore()

    def greet(there):
        pl.semaphore_signal(barrier, inc=1, device_id=there, device_id_type=MESH)

    greet(place(axis, by))
    long = 0
    if detour is None:
        pl.semaphore_wait(barrier, 1)
    else:
        odd = lax.rem(lax.axis_index("row"), 2)
        origin = lax.rem(odd + by, 2)
        long = detour.pick(detour.counts, odd)
        first, second = detour.pick(detour.first, odd), detour.pick(detour.second, odd)
        tiles(as_flag(long), lambda i: greet(place(axis, ROWS - first)))
        tiles(
            as_flag(detour.pick(detour.counts, origin)),
            lambda i: greet(place(axis, ROWS - detour.pick(detour.second, origin))),
        )
        pl.semaphore_wait(barrier, 1 + 2 * as_flag(long))

    def move(i):
        rows = pl.ds(pl.multiple_of(i * piece, piece), piece)
        return pltpu.make_async_remote_copy(
            src_ref=ctx_ref.at[rows],
            dst_ref=land.at[rows],
            send_sem=send.at[i],
            recv_sem=recv.at[i],
            device_id=place(axis, -by),
            device_id_type=MESH,
        )

    def depart(i):
        return pltpu.make_async_remote_copy(
            src_ref=ctx_ref.at[block(PIECES - long + i, piece)],
            dst_ref=hop.at[block(i, piece)],
            send_sem=send.at[PIECES - long + i],
            recv_sem=hop_recv.at[i],
            device_id=place(axis, first),
            device_id_type=MESH,
        )

    def forward(i):
        return pltpu.make_async_remote_copy(
            src_ref=hop.at[block(i, piece)],
            dst_ref=land.at[block(PIECES - long + i, piece)],
            send_sem=hop_send.at[i],
            recv_sem=recv.at[PIECES - long + i],
            device_id=place(axis, second),
            device_id_type=MESH,
        )

    if detour is not None:
        tiles(long, lambda i: depart(i).start())
    tiles(PIECES - long, lambda i: move(i).start())
    source_update(src_in, coef_in, low_in, src_out)

    def narrow(i):
        rows = block(i, STRIP)
        src_low[rows, :] = src_out[rows, :].astype(jnp.bfloat16)

    tiles(size // STRIP, narrow)
    for fetch in fetches:
        fetch.wait()
    lap = lap_ref[0]

    def group(g):
        tiles(GROUP // piece, lambda k: move(g * (GROUP // piece) + k).wait_recv())
        rows = block(g, GROUP)
        low_out[rows, :] = land[rows, :].astype(jnp.bfloat16)

        def score(i):
            strip = block(i, STRIP)
            scores = lax.dot_general(
                src_low[strip, :],
                low_out[rows, :],
                (((1,), (1,)), ((), ())),
                preferred_element_type=jnp.float32,
            )
            count = weight[lap, strip, rows].astype(jnp.float32)
            coef = (count + NEG_WEIGHT) * jax.nn.sigmoid(scores) - count
            coef_out[strip, rows] = coef.astype(jnp.bfloat16)

        tiles(src_low.shape[0] // STRIP, score)
        grad_ref[...] = lax.dot_general(
            coef_out[:, rows],
            src_low[...],
            (((0,), (0,)), ((), ())),
            preferred_element_type=jnp.float32,
        )

        def update(i):
            strip = pl.ds(pl.multiple_of(g * GROUP + i * 32, 32), 32)
            ctx_out[strip, :] = normalized(land[strip, :], grad_ref[block(i, 32), :])

        tiles(GROUP // 32, update)

    if detour is not None:

        def relay(i):
            depart(i).wait_recv()
            forward(i).start()

        tiles(long, relay)
    tiles(size // GROUP, group)
    tiles(PIECES, lambda i: move(i).wait_send())
    if detour is not None:
        tiles(long, lambda i: forward(i).wait_send())


def one_round(axis, by, turns, number, lap, ctx, src, coef, low, counts):
    size, width = ctx.shape
    vmem = pl.BlockSpec(memory_space=pltpu.VMEM)
    out = [jax.ShapeDtypeStruct(x.shape, x.dtype) for x in (ctx, src, coef, low)]
    detour = detour_of(axis, by)
    detour_scratch = []
    if detour is not None:
        most = max(detour.counts)
        detour_scratch = [
            pltpu.VMEM((most * (size // PIECES), width), jnp.float32),
            pltpu.SemaphoreType.DMA((most,)),
            pltpu.SemaphoreType.DMA((most,)),
        ]
    return pl.pallas_call(
        functools.partial(round_kernel, axis, by, turns),
        out_shape=tuple(out),
        in_specs=[pl.BlockSpec(memory_space=pltpu.SMEM)]
        + [vmem] * 4
        + [pl.BlockSpec(memory_space=pl.ANY)],
        out_specs=[vmem] * 4,
        scratch_shapes=[
            pltpu.VMEM((size, width), jnp.float32),
            pltpu.VMEM((len(turns), src.shape[0], size), jnp.int32),
            pltpu.VMEM(src.shape, jnp.bfloat16),
            pltpu.VMEM((GROUP, width), jnp.float32),
            pltpu.SemaphoreType.DMA((PIECES,)),
            pltpu.SemaphoreType.DMA((PIECES,)),
            pltpu.SemaphoreType.DMA((len(turns),)),
        ]
        + detour_scratch,
        name=f"round_{axis}{by}",
        compiler_params=pltpu.CompilerParams(
            collective_id=number, has_side_effects=True, vmem_limit_bytes=24 << 20
        ),
    )(lap, ctx, src, coef, low, counts)


QUARTERS = 4


def home_detour(by):
    detour = Detour(by, (COLS, COLS + COLS // 2))
    return detour if detour.any else None


def return_kernel(by, offsets, ctx_ref, src_in, coef_in, low_in, ctx_out, src_out, *scratch):
    near = scratch[:QUARTERS]
    stage = scratch[QUARTERS : 2 * QUARTERS]
    far = scratch[2 * QUARTERS : 3 * QUARTERS]
    send1, recv1, send2, recv2, *detoured = scratch[3 * QUARTERS :]
    size, width = ctx_ref.shape
    quarter = size // QUARTERS
    piece = quarter // COLS
    row, col = lax.axis_index("row"), lax.axis_index("col")

    def at(row_by, col_by):
        return (lax.rem(row + row_by + ROWS, ROWS), lax.rem(col + col_by + COLS, COLS))

    barrier = pltpu.get_barrier_semaphore()

    def greet(there):
        pl.semaphore_signal(barrier, inc=1, device_id=there, device_id_type=MESH)

    start = 0 if by else 1
    tiles(COLS - start, lambda i: greet(at(-by, -i - start)))
    if by:
        tiles(COLS - 1, lambda i: greet(at(0, -i - 1)))
    met = COLS - start + (COLS - 1 if by else 0)
    detour = home_detour(by)
    long = 0
    if detour is not None:
        hop, hop_send, hop_recv = detoured
        odd = lax.rem(row, 2)
        origin = lax.rem(odd + by, 2)
        long = detour.pick(detour.counts, odd)
        first, second = detour.pick(detour.first, odd), detour.pick(detour.second, odd)
        tiles(as_flag(long), lambda i: greet(at(-first, 0)))
        back = detour.pick(detour.second, origin)
        tiles(
            as_flag(detour.pick(detour.counts, origin)) * COLS,
            lambda i: greet(at(-back, -i)),
        )
        met = met + (COLS + 1) * as_flag(long)
    pl.semaphore_wait(barrier, met)

    def spread(q, i):
        return pltpu.make_async_remote_copy(
            src_ref=ctx_ref.at[pl.ds(pl.multiple_of(q * quarter + i * piece, piece), piece)],
            dst_ref=near[q].at[i],
            send_sem=send1.at[q],
            recv_sem=recv1.at[q],
            device_id=at(by, i),
            device_id_type=MESH,
        )

    def spread_all(q):
        own = pl.ds(q * quarter + start * piece, quarter - start * piece)
        return pltpu.make_async_remote_copy(
            src_ref=ctx_ref.at[own],
            dst_ref=near[q].at[pl.ds(start, COLS - start)],
            send_sem=send1.at[q],
            recv_sem=recv1.at[q],
            device_id=at(by, 1),
            device_id_type=MESH,
        )

    def deliver_all(q):
        return pltpu.make_async_remote_copy(
            src_ref=stage[q].at[pl.ds(1, COLS - 1)],
            dst_ref=far[q].at[pl.ds(1, COLS - 1)],
            send_sem=send2.at[q],
            recv_sem=recv2.at[q],
            device_id=at(0, 1),
            device_id_type=MESH,
        )

    def deliver(q, i):
        return pltpu.make_async_remote_copy(
            src_ref=stage[q].at[i],
            dst_ref=far[q].at[i],
            send_sem=send2.at[q],
            recv_sem=recv2.at[q],
            device_id=at(0, i),
            device_id_type=MESH,
        )

    half = quarter // 2

    def depart(q, part):
        return pltpu.make_async_remote_copy(
            src_ref=ctx_ref.at[pl.ds(q * quarter + part * half, half)],
            dst_ref=hop[q % 2].at[pl.ds(part * half, half)],
            send_sem=send1.at[q],
            recv_sem=hop_recv.at[q % 2 * 2 + part],
            device_id=at(first, 0),
            device_id_type=MESH,
        )

    def relay(q, part, i):
        return pltpu.make_async_remote_copy(
            src_ref=hop[q % 2].at[pl.ds(pl.multiple_of(i * piece, piece), piece)],
            dst_ref=near[q].at[i],
            send_sem=hop_send.at[q % 2 * 2 + part],
            recv_sem=recv1.at[q],
            device_id=at(second, i),
            device_id_type=MESH,
        )

    def relayed(q, part):
        return pltpu.make_async_remote_copy(
            src_ref=hop[q % 2].at[pl.ds(part * half, half)],
            dst_ref=near[q].at[pl.ds(part * (COLS // 2), COLS // 2)],
            send_sem=hop_send.at[q % 2 * 2 + part],
            recv_sem=recv1.at[q],
            device_id=at(second, 1),
            device_id_type=MESH,
        )

    ways = []
    if detour is not None:
        ways = [(3, 0, as_flag(long)), (3, 1, as_flag(long)), (2, 1, as_flag(long // (COLS + 1)))]
    for q, part, flag in ways:
        tiles(flag, lambda i, q=q, part=part: depart(q, part).start())
    for q in range(QUARTERS):
        direct = COLS - start
        for other, part, flag in ways:
            if other == q:
                direct = direct - flag * (COLS // 2)
        tiles(direct, lambda i, q=q: spread(q, i + start).start())
        if not by:
            near[q][0] = ctx_ref[pl.ds(q * quarter, piece), :]
    source_update(src_in, coef_in, low_in, src_out)
    for q, part, flag in ways:

        def pass_relay(i, q=q, part=part):
            depart(q, part).wait_recv()
            tiles(COLS // 2, lambda k: relay(q, part, part * (COLS // 2) + k).start())

        tiles(flag, pass_relay)
    shift = offsets[1]
    for turn in range(3, offsets.shape[0], 2):
        shift = shift + offsets[turn]
    shift = lax.rem(shift, COLS)
    for q in range(QUARTERS):
        spread_all(q).wait_recv()
        far[q][0] = near[q][lax.rem(shift, COLS)]

        def pass_on(i, q=q):
            stage[q][i + 1] = near[q][lax.rem(shift - i - 1 + COLS, COLS)]
            deliver(q, i + 1).start()

        tiles(COLS - 1, pass_on)
    for q in range(QUARTERS):
        deliver_all(q).wait_recv()

        def settle(i, q=q):
            rows = pl.ds(pl.multiple_of(q * quarter + i * piece, piece), piece)
            ctx_out[rows, :] = far[q][lax.rem(shift - i + COLS, COLS)]

        tiles(COLS, settle)
    for q in range(QUARTERS):
        deliver_all(q).wait_send()
        spread_all(q).wait_send()
    for q, part, flag in ways:
        tiles(flag, lambda i, q=q, part=part: relayed(q, part).wait_send())


def go_home(by, number, offsets, ctx, src, coef, low):
    size, width = ctx.shape
    quarter = size // QUARTERS
    vmem = pl.BlockSpec(memory_space=pltpu.VMEM)
    full = jax.ShapeDtypeStruct((size, width), jnp.float32)
    slots = pltpu.VMEM((COLS, quarter // COLS, width), jnp.float32)
    detoured = []
    if home_detour(by) is not None:
        detoured = [
            [pltpu.VMEM((quarter, width), jnp.float32)] * 2,
            pltpu.SemaphoreType.DMA((4,)),
            pltpu.SemaphoreType.DMA((4,)),
        ]
    return pl.pallas_call(
        functools.partial(return_kernel, by),
        out_shape=(full, full),
        in_specs=[pl.BlockSpec(memory_space=pltpu.SMEM)] + [vmem] * 4,
        out_specs=[vmem] * 2,
        scratch_shapes=[slots] * (3 * QUARTERS)
        + [pltpu.SemaphoreType.DMA((QUARTERS,))] * 4
        + detoured,
        name=f"home{by}",
        compiler_params=pltpu.CompilerParams(
            collective_id=number, has_side_effects=True, vmem_limit_bytes=24 << 20
        ),
    )(offsets, ctx, src, coef, low)


def open_kernel(ctx_ref, src_ref, ctx_out, src_out, coef_out, low_out, sems):
    copies = [
        pltpu.make_async_copy(ctx_ref, ctx_out, sems.at[0]),
        pltpu.make_async_copy(src_ref, src_out, sems.at[1]),
    ]
    for copy in copies:
        copy.start()

    def clear(i):
        rows = block(i, STRIP)
        coef_out[rows, :] = jnp.zeros((STRIP, coef_out.shape[1]), coef_out.dtype)
        low_out[rows, :] = jnp.zeros((STRIP, low_out.shape[1]), low_out.dtype)

    tiles(coef_out.shape[0] // STRIP, clear)
    for copy in copies:
        copy.wait()


def opened(ctx, src):
    vmem = pl.BlockSpec(memory_space=pltpu.VMEM)
    hbm = pl.BlockSpec(memory_space=pl.ANY)
    return pl.pallas_call(
        open_kernel,
        out_shape=(
            jax.ShapeDtypeStruct(ctx.shape, ctx.dtype),
            jax.ShapeDtypeStruct(src.shape, src.dtype),
            jax.ShapeDtypeStruct((src.shape[0], ctx.shape[0]), jnp.bfloat16),
            jax.ShapeDtypeStruct(ctx.shape, jnp.bfloat16),
        ),
        in_specs=[hbm, hbm],
        out_specs=[pl.BlockSpec(memory_space=pltpu.VMEM), pl.BlockSpec(memory_space=pltpu.VMEM), vmem, vmem],
        scratch_shapes=[pltpu.SemaphoreType.DMA((2,))],
        name="opened",
    )(ctx, src)


def per_device(source, context, pair_counts, partner_masks):
    rounds = pair_counts.shape[0]

    picks = partner_masks - 1

    def both(lap, carried):
        pair = lax.dynamic_slice_in_dim(picks, 2 * lap, 2, allow_negative_indices=False)
        for half, (axis, length) in enumerate((("row", ROWS), ("col", COLS))):
            branches = [
                functools.partial(
                    one_round, axis, by, range(half, rounds, 2), half * ROWS + by
                )
                for by in range(1, length)
            ]
            carried = lax.switch(pair[half], branches, lap.reshape(1), *carried, pair_counts)
        return tuple(carried)

    ctx, src, coef, low = lax.fori_loop(0, rounds // 2, both, opened(context, source))
    row_total = sum(partner_masks[turn] for turn in range(0, rounds, 2)) & (ROWS - 1)
    branches = [functools.partial(go_home, by, 2 * ROWS + by) for by in range(ROWS)]
    ctx, src = lax.switch(row_total, branches, partner_masks, ctx, src, coef, low)
    return (src, ctx)


def solution(mesh):
    in_specs = (
        P(("row", "col"), None),
        P(("row", "col"), None),
        P(None, ("row", "col"), None),
        P(),
    )
    out_specs = (P(("row", "col"), None), P(("row", "col"), None))
    return jax.shard_map(
        per_device, mesh=mesh, in_specs=in_specs, out_specs=out_specs, check_vma=False
    )
```

```python
import functools

import jax
import jax.numpy as jnp
from jax import lax
from jax.experimental import pallas as pl
from jax.experimental.pallas import tpu as pltpu
from jax.sharding import PartitionSpec as P

LEARN_RATE = 0.05
NEG_WEIGHT = 1.0
EPSILON = 1e-06
MESH = pl.DeviceIdType.MESH
ROWS = 16
COLS = 16
GROUP = 128
PIECES = 16
STRIP = 64


def normalized(param, grad):
    scale = lax.rsqrt(jnp.mean(grad * grad, axis=1, keepdims=True) + EPSILON)
    return param - LEARN_RATE * grad * scale


def place(axis, by):
    row, col = lax.axis_index("row"), lax.axis_index("col")
    if axis == "row":
        return (lax.rem(row + by + ROWS, ROWS), col)
    return (row, lax.rem(col + by + COLS, COLS))


class Detour:
    def __init__(self, shift, parts):
        counts, first, second = [], [], []
        for odd in range(2):
            hops = ((odd + shift) // 2) % 8
            hops = hops - 8 if hops > 4 else hops
            sign = 1 if hops > 0 else -1
            leg = {2: -3 * sign, 3: -2 * sign}.get(abs(hops), 0)
            counts.append({2: parts[0], 3: parts[1]}.get(abs(hops), 0))
            first.append(2 * leg % ROWS)
            second.append((shift - 2 * leg) % ROWS)
        self.shift, self.counts, self.first, self.second = shift, counts, first, second
        self.any = max(counts) > 0

    @staticmethod
    def pick(values, odd):
        return values[0] if values[0] == values[1] else values[0] + (values[1] - values[0]) * odd


def tiles(count, body):
    def step(i, carry):
        body(i)
        return carry

    lax.fori_loop(0, count, step, 0)


def block(i, size):
    return pl.ds(pl.multiple_of(i * size, size), size)


def source_update(src_ref, coef_ref, low_ref, src_out):
    def step(i):
        rows = block(i, STRIP)
        grad = jnp.dot(coef_ref[rows, :], low_ref[...], preferred_element_type=jnp.float32)
        src_out[rows, :] = normalized(src_ref[rows, :], grad)

    tiles(src_ref.shape[0] // STRIP, step)


def as_flag(count):
    return jnp.minimum(count, 1)


def detour_of(axis, by):
    if axis != "row":
        return None
    detour = Detour(-by, (4, 6))
    return detour if detour.any else None


def round_kernel(
    axis,
    by,
    turns,
    lap_ref,
    ctx_ref,
    src_in,
    coef_in,
    low_in,
    counts,
    ctx_out,
    src_out,
    coef_out,
    low_out,
    land,
    weight,
    src_low,
    grad_ref,
    send,
    recv,
    wsem,
    hop=None,
    hop_send=None,
    hop_recv=None,
):
    size = ctx_ref.shape[0]
    piece = size // PIECES
    fetches = [
        pltpu.make_async_copy(counts.at[turn], weight.at[lap], wsem.at[lap])
        for lap, turn in enumerate(turns)
    ]
    for fetch in fetches:
        fetch.start()
    detour = detour_of(axis, by)
    barrier = pltpu.get_barrier_semaphore()

    def greet(there):
        pl.semaphore_signal(barrier, inc=1, device_id=there, device_id_type=MESH)

    greet(place(axis, by))
    long = 0
    if detour is None:
        pl.semaphore_wait(barrier, 1)
    else:
        odd = lax.rem(lax.axis_index("row"), 2)
        origin = lax.rem(odd + by, 2)
        long = detour.pick(detour.counts, odd)
        first, second = detour.pick(detour.first, odd), detour.pick(detour.second, odd)
        tiles(as_flag(long), lambda i: greet(place(axis, ROWS - first)))
        tiles(
            as_flag(detour.pick(detour.counts, origin)),
            lambda i: greet(place(axis, ROWS - detour.pick(detour.second, origin))),
        )
        pl.semaphore_wait(barrier, 1 + 2 * as_flag(long))

    def move(i):
        rows = pl.ds(pl.multiple_of(i * piece, piece), piece)
        return pltpu.make_async_remote_copy(
            src_ref=ctx_ref.at[rows],
            dst_ref=land.at[rows],
            send_sem=send.at[i],
            recv_sem=recv.at[i],
            device_id=place(axis, -by),
            device_id_type=MESH,
        )

    def depart(i):
        return pltpu.make_async_remote_copy(
            src_ref=ctx_ref.at[block(PIECES - long + i, piece)],
            dst_ref=hop.at[block(i, piece)],
            send_sem=send.at[PIECES - long + i],
            recv_sem=hop_recv.at[i],
            device_id=place(axis, first),
            device_id_type=MESH,
        )

    def forward(i):
        return pltpu.make_async_remote_copy(
            src_ref=hop.at[block(i, piece)],
            dst_ref=land.at[block(PIECES - long + i, piece)],
            send_sem=hop_send.at[i],
            recv_sem=recv.at[PIECES - long + i],
            device_id=place(axis, second),
            device_id_type=MESH,
        )

    if detour is not None:
        tiles(long, lambda i: depart(i).start())
    tiles(PIECES - long, lambda i: move(i).start())
    source_update(src_in, coef_in, low_in, src_out)

    def narrow(i):
        rows = block(i, STRIP)
        src_low[rows, :] = src_out[rows, :].astype(jnp.bfloat16)

    tiles(size // STRIP, narrow)
    for fetch in fetches:
        fetch.wait()
    lap = lap_ref[0]

    def group(g):
        tiles(GROUP // piece, lambda k: move(g * (GROUP // piece) + k).wait_recv())
        rows = block(g, GROUP)
        low_out[rows, :] = land[rows, :].astype(jnp.bfloat16)

        def score(i):
            strip = block(i, STRIP)
            scores = lax.dot_general(
                src_low[strip, :],
                low_out[rows, :],
                (((1,), (1,)), ((), ())),
                preferred_element_type=jnp.float32,
            )
            count = weight[lap, strip, rows].astype(jnp.float32)
            coef = (count + NEG_WEIGHT) * jax.nn.sigmoid(scores) - count
            coef_out[strip, rows] = coef.astype(jnp.bfloat16)

        tiles(src_low.shape[0] // STRIP, score)
        grad_ref[...] = lax.dot_general(
            coef_out[:, rows],
            src_low[...],
            (((0,), (0,)), ((), ())),
            preferred_element_type=jnp.float32,
        )

        def update(i):
            strip = pl.ds(pl.multiple_of(g * GROUP + i * 32, 32), 32)
            ctx_out[strip, :] = normalized(land[strip, :], grad_ref[block(i, 32), :])

        tiles(GROUP // 32, update)

    if detour is not None:

        def relay(i):
            depart(i).wait_recv()
            forward(i).start()

        tiles(long, relay)
    tiles(size // GROUP, group)
    tiles(PIECES, lambda i: move(i).wait_send())
    if detour is not None:
        tiles(long, lambda i: forward(i).wait_send())


def one_round(axis, by, turns, number, lap, ctx, src, coef, low, counts):
    size, width = ctx.shape
    vmem = pl.BlockSpec(memory_space=pltpu.VMEM)
    out = [jax.ShapeDtypeStruct(x.shape, x.dtype) for x in (ctx, src, coef, low)]
    detour = detour_of(axis, by)
    detour_scratch = []
    if detour is not None:
        most = max(detour.counts)
        detour_scratch = [
            pltpu.VMEM((most * (size // PIECES), width), jnp.float32),
            pltpu.SemaphoreType.DMA((most,)),
            pltpu.SemaphoreType.DMA((most,)),
        ]
    return pl.pallas_call(
        functools.partial(round_kernel, axis, by, turns),
        out_shape=tuple(out),
        in_specs=[pl.BlockSpec(memory_space=pltpu.SMEM)]
        + [vmem] * 4
        + [pl.BlockSpec(memory_space=pl.ANY)],
        out_specs=[vmem] * 4,
        scratch_shapes=[
            pltpu.VMEM((size, width), jnp.float32),
            pltpu.VMEM((len(turns), src.shape[0], size), jnp.int32),
            pltpu.VMEM(src.shape, jnp.bfloat16),
            pltpu.VMEM((GROUP, width), jnp.float32),
            pltpu.SemaphoreType.DMA((PIECES,)),
            pltpu.SemaphoreType.DMA((PIECES,)),
            pltpu.SemaphoreType.DMA((len(turns),)),
        ]
        + detour_scratch,
        name=f"round_{axis}{by}",
        compiler_params=pltpu.CompilerParams(
            collective_id=number, has_side_effects=True, vmem_limit_bytes=24 << 20
        ),
    )(lap, ctx, src, coef, low, counts)


QUARTERS = 4


def home_detour(by):
    detour = Detour(by, (COLS, COLS + COLS // 2))
    return detour if detour.any else None


def return_kernel(by, offsets, ctx_ref, src_in, coef_in, low_in, ctx_out, src_out, *scratch):
    near = scratch[:QUARTERS]
    stage = scratch[QUARTERS : 2 * QUARTERS]
    far = scratch[2 * QUARTERS : 3 * QUARTERS]
    send1, recv1, send2, recv2, *detoured = scratch[3 * QUARTERS :]
    size, width = ctx_ref.shape
    quarter = size // QUARTERS
    piece = quarter // COLS
    row, col = lax.axis_index("row"), lax.axis_index("col")

    def at(row_by, col_by):
        return (lax.rem(row + row_by + ROWS, ROWS), lax.rem(col + col_by + COLS, COLS))

    barrier = pltpu.get_barrier_semaphore()

    def greet(there):
        pl.semaphore_signal(barrier, inc=1, device_id=there, device_id_type=MESH)

    start = 0 if by else 1
    tiles(COLS - start, lambda i: greet(at(-by, -i - start)))
    if by:
        tiles(COLS - 1, lambda i: greet(at(0, -i - 1)))
    met = COLS - start + (COLS - 1 if by else 0)
    detour = home_detour(by)
    long = 0
    if detour is not None:
        hop, hop_send, hop_recv = detoured
        odd = lax.rem(row, 2)
        origin = lax.rem(odd + by, 2)
        long = detour.pick(detour.counts, odd)
        first, second = detour.pick(detour.first, odd), detour.pick(detour.second, odd)
        tiles(as_flag(long), lambda i: greet(at(-first, 0)))
        back = detour.pick(detour.second, origin)
        tiles(
            as_flag(detour.pick(detour.counts, origin)) * COLS,
            lambda i: greet(at(-back, -i)),
        )
        met = met + (COLS + 1) * as_flag(long)
    pl.semaphore_wait(barrier, met)

    def spread(q, i):
        return pltpu.make_async_remote_copy(
            src_ref=ctx_ref.at[pl.ds(pl.multiple_of(q * quarter + i * piece, piece), piece)],
            dst_ref=near[q].at[i],
            send_sem=send1.at[q],
            recv_sem=recv1.at[q],
            device_id=at(by, i),
            device_id_type=MESH,
        )

    def spread_all(q):
        own = pl.ds(q * quarter + start * piece, quarter - start * piece)
        return pltpu.make_async_remote_copy(
            src_ref=ctx_ref.at[own],
            dst_ref=near[q].at[pl.ds(start, COLS - start)],
            send_sem=send1.at[q],
            recv_sem=recv1.at[q],
            device_id=at(by, 1),
            device_id_type=MESH,
        )

    def deliver_all(q):
        return pltpu.make_async_remote_copy(
            src_ref=stage[q].at[pl.ds(1, COLS - 1)],
            dst_ref=far[q].at[pl.ds(1, COLS - 1)],
            send_sem=send2.at[q],
            recv_sem=recv2.at[q],
            device_id=at(0, 1),
            device_id_type=MESH,
        )

    def deliver(q, i):
        return pltpu.make_async_remote_copy(
            src_ref=stage[q].at[i],
            dst_ref=far[q].at[i],
            send_sem=send2.at[q],
            recv_sem=recv2.at[q],
            device_id=at(0, i),
            device_id_type=MESH,
        )

    half = quarter // 2

    def depart(q, part):
        return pltpu.make_async_remote_copy(
            src_ref=ctx_ref.at[pl.ds(q * quarter + part * half, half)],
            dst_ref=hop[q % 2].at[pl.ds(part * half, half)],
            send_sem=send1.at[q],
            recv_sem=hop_recv.at[q % 2 * 2 + part],
            device_id=at(first, 0),
            device_id_type=MESH,
        )

    def relay(q, part, i):
        return pltpu.make_async_remote_copy(
            src_ref=hop[q % 2].at[pl.ds(pl.multiple_of(i * piece, piece), piece)],
            dst_ref=near[q].at[i],
            send_sem=hop_send.at[q % 2 * 2 + part],
            recv_sem=recv1.at[q],
            device_id=at(second, i),
            device_id_type=MESH,
        )

    def relayed(q, part):
        return pltpu.make_async_remote_copy(
            src_ref=hop[q % 2].at[pl.ds(part * half, half)],
            dst_ref=near[q].at[pl.ds(part * (COLS // 2), COLS // 2)],
            send_sem=hop_send.at[q % 2 * 2 + part],
            recv_sem=recv1.at[q],
            device_id=at(second, 1),
            device_id_type=MESH,
        )

    ways = []
    if detour is not None:
        ways = [(3, 0, as_flag(long)), (3, 1, as_flag(long)), (2, 1, as_flag(long // (COLS + 1)))]
    for q, part, flag in ways:
        tiles(flag, lambda i, q=q, part=part: depart(q, part).start())
    for q in range(QUARTERS):
        direct = COLS - start
        for other, part, flag in ways:
            if other == q:
                direct = direct - flag * (COLS // 2)
        tiles(direct, lambda i, q=q: spread(q, i + start).start())
        if not by:
            near[q][0] = ctx_ref[pl.ds(q * quarter, piece), :]
    source_update(src_in, coef_in, low_in, src_out)
    for q, part, flag in ways:

        def pass_relay(i, q=q, part=part):
            depart(q, part).wait_recv()
            tiles(COLS // 2, lambda k: relay(q, part, part * (COLS // 2) + k).start())

        tiles(flag, pass_relay)
    shift = offsets[1]
    for turn in range(3, offsets.shape[0], 2):
        shift = shift + offsets[turn]
    shift = lax.rem(shift, COLS)
    for q in range(QUARTERS):
        spread_all(q).wait_recv()
        far[q][0] = near[q][lax.rem(shift, COLS)]

        def pass_on(i, q=q):
            stage[q][i + 1] = near[q][lax.rem(shift - i - 1 + COLS, COLS)]
            deliver(q, i + 1).start()

        tiles(COLS - 1, pass_on)
    for q in range(QUARTERS):
        deliver_all(q).wait_recv()

        def settle(i, q=q):
            rows = pl.ds(pl.multiple_of(q * quarter + i * piece, piece), piece)
            ctx_out[rows, :] = far[q][lax.rem(shift - i + COLS, COLS)]

        tiles(COLS, settle)
    for q in range(QUARTERS):
        deliver_all(q).wait_send()
        spread_all(q).wait_send()
    for q, part, flag in ways:
        tiles(flag, lambda i, q=q, part=part: relayed(q, part).wait_send())


def go_home(by, number, offsets, ctx, src, coef, low):
    size, width = ctx.shape
    quarter = size // QUARTERS
    vmem = pl.BlockSpec(memory_space=pltpu.VMEM)
    full = jax.ShapeDtypeStruct((size, width), jnp.float32)
    slots = pltpu.VMEM((COLS, quarter // COLS, width), jnp.float32)
    detoured = []
    if home_detour(by) is not None:
        detoured = [
            [pltpu.VMEM((quarter, width), jnp.float32)] * 2,
            pltpu.SemaphoreType.DMA((4,)),
            pltpu.SemaphoreType.DMA((4,)),
        ]
    return pl.pallas_call(
        functools.partial(return_kernel, by),
        out_shape=(full, full),
        in_specs=[pl.BlockSpec(memory_space=pltpu.SMEM)] + [vmem] * 4,
        out_specs=[vmem] * 2,
        scratch_shapes=[slots] * (3 * QUARTERS)
        + [pltpu.SemaphoreType.DMA((QUARTERS,))] * 4
        + detoured,
        name=f"home{by}",
        compiler_params=pltpu.CompilerParams(
            collective_id=number, has_side_effects=True, vmem_limit_bytes=24 << 20
        ),
    )(offsets, ctx, src, coef, low)


def open_kernel(
    offsets, ctx_ref, src_ref, ctx_out, src_out, coef_out, low_out, row_total, sems
):
    total = offsets[0]
    for turn in range(2, offsets.shape[0], 2):
        total = total + offsets[turn]
    row_total[0] = lax.rem(total, ROWS)
    copies = [
        pltpu.make_async_copy(ctx_ref, ctx_out, sems.at[0]),
        pltpu.make_async_copy(src_ref, src_out, sems.at[1]),
    ]
    for copy in copies:
        copy.start()

    def clear(i):
        rows = block(i, STRIP)
        coef_out[rows, :] = jnp.zeros((STRIP, coef_out.shape[1]), coef_out.dtype)
        low_out[rows, :] = jnp.zeros((STRIP, low_out.shape[1]), low_out.dtype)

    tiles(coef_out.shape[0] // STRIP, clear)
    for copy in copies:
        copy.wait()


def opened(offsets, ctx, src):
    vmem = pl.BlockSpec(memory_space=pltpu.VMEM)
    hbm = pl.BlockSpec(memory_space=pl.ANY)
    smem = pl.BlockSpec(memory_space=pltpu.SMEM)
    return pl.pallas_call(
        open_kernel,
        out_shape=(
            jax.ShapeDtypeStruct(ctx.shape, ctx.dtype),
            jax.ShapeDtypeStruct(src.shape, src.dtype),
            jax.ShapeDtypeStruct((src.shape[0], ctx.shape[0]), jnp.bfloat16),
            jax.ShapeDtypeStruct(ctx.shape, jnp.bfloat16),
            jax.ShapeDtypeStruct((1,), jnp.int32),
        ),
        in_specs=[smem, hbm, hbm],
        out_specs=[pl.BlockSpec(memory_space=pltpu.VMEM), pl.BlockSpec(memory_space=pltpu.VMEM), vmem, vmem, smem],
        scratch_shapes=[pltpu.SemaphoreType.DMA((2,))],
        name="opened",
    )(offsets, ctx, src)


def per_device(source, context, pair_counts, partner_masks):
    rounds = pair_counts.shape[0]

    picks = partner_masks - 1

    def both(lap, carried):
        pair = lax.dynamic_slice_in_dim(picks, 2 * lap, 2, allow_negative_indices=False)
        for half, (axis, length) in enumerate((("row", ROWS), ("col", COLS))):
            branches = [
                functools.partial(
                    one_round, axis, by, range(half, rounds, 2), half * ROWS + by
                )
                for by in range(1, length)
            ]
            carried = lax.switch(pair[half], branches, lap.reshape(1), *carried, pair_counts)
        return tuple(carried)

    *start, row_total = opened(partner_masks, context, source)
    ctx, src, coef, low = lax.fori_loop(0, rounds // 2, both, tuple(start))
    branches = [functools.partial(go_home, by, 2 * ROWS + by) for by in range(ROWS)]
    ctx, src = lax.switch(row_total.reshape(()), branches, partner_masks, ctx, src, coef, low)
    return (src, ctx)


def solution(mesh):
    in_specs = (
        P(("row", "col"), None),
        P(("row", "col"), None),
        P(None, ("row", "col"), None),
        P(),
    )
    out_specs = (P(("row", "col"), None), P(("row", "col"), None))
    return jax.shard_map(
        per_device, mesh=mesh, in_specs=in_specs, out_specs=out_specs, check_vma=False
    )
```
